32 devices in a mesh: scene: 4 (over y, x), expo: 8 (over z, core).
Axes of the slice: x: 2, y: 2, z: 4, core: 2. Of those that a mesh axis runs over, the one named last changes fastest.
Arguments:
- scene: bfloat16 [2048, 128, 128], P(('scene', 'expo')), may hold values from -6 to 6
- observed: bfloat16 [1024, 128, 128], P('expo'), may hold values from -9 to 9
- inverse_variance: bfloat16 [1024, 128, 128], P('expo'), may hold values from 0.25 to 4
- intersection: int32 [1024, 3], P('expo'), may hold values from 0 to 2047, as said below
- resample_index: int32 [1024, 6], P('expo'), may hold values from 0 to 31
- psf_index: int32 [1024], P('expo'), may hold values from 0 to 15
- resample_bank: bfloat16 [32, 128, 128], replicated, may hold values from -0.5 to 0.5
- psf_bank: bfloat16 [16, 128, 128], replicated, may hold values from -0.5 to 0.5
Outputs:
- gradient: float32 [2048, 128, 128], P(('scene', 'expo'))
The draws below stay inside these ranges and needn't reach their ends.
Inputs may be any that keep to these rules, and one draw needn't show every extreme that they name: `intersection`: the 3 scene blocks of exposure block j have 3 different owners and lie in sky strips j // 128 - 1 to j // 128 + 1; for each sky strip of exposure blocks, one owner appears in every one of its blocks.
All inputs are finite; a program needn't handle non-finite values.
Results may differ from the reference program's by a relative error of at most 0.014.
Values may be sent and summed in bfloat16 or wider, within the bound.
A program may use at most 128 MiB of HBM per device.

```python
import math
import jax
import jax.numpy as jnp
from jax import lax

P_SIZE = 128
K = 3
NW = 32
NPSF = 16
SB_DEV = 64
EB_DEV = 128
OWNERS = 4
STRIPS = 8
SB = 2048
EB = 1024


def draw_intersection(key, part):
    keys = jax.random.split(key, 6)
    blocks = jnp.arange(EB, dtype=jnp.int32)
    home = blocks // EB_DEV
    hot = jax.random.randint(keys[0], (STRIPS,), 0, OWNERS)[home]
    first = jax.random.randint(keys[1], (EB,), 1, OWNERS)
    second = jax.random.randint(keys[2], (EB,), 1, OWNERS - 1)
    second = jnp.where(second >= first, second + 1, second)
    owners_all = jnp.stack([hot, (hot + first) % OWNERS, (hot + second) % OWNERS], axis=1)
    turn = jax.random.randint(keys[3], (EB,), 0, K)
    order = (jnp.arange(K, dtype=jnp.int32)[None, :] + turn[:, None]) % K
    owners_all = jnp.take_along_axis(owners_all, order, axis=1)
    step_strip = jax.random.randint(keys[4], (EB, K), -1, 2)
    target = jnp.clip(home[:, None] + step_strip, 0, STRIPS - 1)
    within = jax.random.randint(keys[5], (EB, K), 0, SB_DEV)
    return (owners_all * (STRIPS * SB_DEV) + target * SB_DEV + within).astype(jnp.int32)


def plant(result, own_key, low, high):
    longest = result.shape.index(max(result.shape))
    spots = []
    for shift in (0, 1):
        where = [jax.random.randint(jax.random.fold_in(own_key, axis), (), 0, length) for axis, length in enumerate(result.shape)]
        where[longest] = (where[longest] + shift) % result.shape[longest]
        spots.append(tuple(where))
    return result.at[spots[0]].set(low).at[spots[1]].set(high)


def steps_of(stream_key, shape, shards, low, high):
    level = 1.0
    for dim, parts in shards:
        draws = jax.random.uniform(jax.random.fold_in(jax.random.fold_in(stream_key, 6), dim), (parts,), jnp.float32, low / len(shards), high / len(shards))
        level = level * jnp.repeat(jnp.exp(draws), shape[dim] // parts).reshape((-1,) + (1,) * (len(shape) - 1 - dim))
    return level


def gaussian(key, dims, deviation, reach, cuts=(), held_as=jnp.bfloat16):
    values = deviation * jax.random.normal(key, dims, jnp.float32)
    if cuts:
        values = values * steps_of(key, dims, cuts, -0.22, 0.18)
    return jnp.clip(values, -reach, reach).astype(held_as)


def setup_inputs(seed: int = 0) -> dict:
    seeds = jax.random.split(jax.random.key(seed), 9)
    return {
        "scene": gaussian(seeds[0], (SB, P_SIZE, P_SIZE), 1.0, 6.0, ((0, 32),)),
        "observed": gaussian(seeds[1], (EB, P_SIZE, P_SIZE), 1.5, 9.0, ((0, 8),)),
        "inverse_variance": jnp.clip(jnp.exp(math.log(4.0) - 2.7725887 * jax.random.uniform(seeds[2], (EB, P_SIZE, P_SIZE), jnp.float32) ** steps_of(seeds[2], (EB, P_SIZE, P_SIZE), ((0, 8),), -0.2, 0.2)), 0.25, 4.0).astype(jnp.bfloat16),
        "intersection": draw_intersection(jax.random.fold_in(seeds[8], 71), 0),
        "resample_index": plant(jax.random.randint(seeds[4], (EB, 2 * K), 0, NW), jax.random.fold_in(seeds[4], 1), 0, NW - 1).astype(jnp.int32),
        "psf_index": plant(jax.random.randint(seeds[5], (EB,), 0, NPSF), jax.random.fold_in(seeds[5], 1), 0, NPSF - 1).astype(jnp.int32),
        "resample_bank": gaussian(seeds[6], (NW, P_SIZE, P_SIZE), P_SIZE ** -0.5, 0.5),
        "psf_bank": gaussian(seeds[7], (NPSF, P_SIZE, P_SIZE), P_SIZE ** -0.5, 0.5),
    }


def reference(scene, observed, inverse_variance, intersection, resample_index, psf_index, resample_bank, psf_bank):
    total = jnp.zeros((EB, P_SIZE, P_SIZE), jnp.float32)
    for k in range(K):
        blocks = scene[intersection[:, k]].astype(jnp.float32)
        rows = resample_bank[resample_index[:, k]].astype(jnp.float32)
        cols = resample_bank[resample_index[:, K + k]].astype(jnp.float32)
        inner = jnp.einsum('jab,jcb->jac', blocks, cols).astype(jnp.bfloat16).astype(jnp.float32)
        term = jnp.einsum('jca,jab->jcb', rows, inner).astype(jnp.bfloat16)
        total = total + lax.optimization_barrier(term).astype(jnp.float32)
    resampled = total.astype(jnp.bfloat16).astype(jnp.float32)
    blur = psf_bank[psf_index].astype(jnp.float32)
    blurred_half = jnp.einsum('jab,jcb->jac', resampled, blur).astype(jnp.bfloat16).astype(jnp.float32)
    model = jnp.einsum('jca,jab->jcb', blur, blurred_half)
    weighted = (inverse_variance.astype(jnp.float32) * (model - observed.astype(jnp.float32))).astype(jnp.bfloat16).astype(jnp.float32)
    back_half = jnp.einsum('jab,jbc->jac', weighted, blur).astype(jnp.bfloat16).astype(jnp.float32)
    adjoint = jnp.einsum('jba,jbc->jac', blur, back_half).astype(jnp.bfloat16).astype(jnp.float32)
    gradient = jnp.zeros((SB, P_SIZE, P_SIZE), jnp.float32)
    for k in range(K):
        rows = resample_bank[resample_index[:, k]].astype(jnp.float32)
        cols = resample_bank[resample_index[:, K + k]].astype(jnp.float32)
        spread = jnp.einsum('jab,jbc->jac', adjoint, cols).astype(jnp.bfloat16).astype(jnp.float32)
        pulled = jnp.einsum('jba,jbc->jac', rows, spread)
        gradient = gradient.at[intersection[:, k]].add(pulled)
    return gradient
```

```python
import functools

import jax
import jax.numpy as jnp
from jax import lax
from jax.experimental import pallas as pl
from jax.experimental.pallas import tpu as pltpu
from jax.sharding import PartitionSpec as P

MESH = pl.DeviceIdType.MESH
UNROLL = 4
VMEM_LIMIT = 60 * 1024 * 1024


def dot(a, b, dims):
    return lax.dot_general(a, b, (dims, ((), ())), preferred_element_type=jnp.float32)


NN = ((1,), (0,))
NT = ((1,), (1,))
TN = ((0,), (0,))


def passed_along(value, axis, steps):
    count = lax.axis_size(axis)
    initial, last = (max(0, -steps), min(count, count - steps))
    return lax.ppermute(value, axis, [(source, source + steps) for source in range(initial, last)])


class Plan:
    def __init__(self, owners, exposures):
        self.n = owners
        self.bits = owners.bit_length() - 1
        assert 1 << self.bits == owners
        self.half = exposures // 2
        self.m = self.half // owners
        self.c = min(8, self.m)
        self.chunks = self.m // self.c

    def bit(self, h, p):
        return p if h == 0 else self.bits - 1 - p

    def value(self, owner, h, p):
        return (owner // (1 << self.bit(h, p))) % 2

    def partner(self, owner, h, p):
        step = 1 << self.bit(h, p)
        return owner + step - 2 * step * self.value(owner, h, p)

    def unit(self, owner, h, t):
        u = 0
        for p in range(self.bits):
            weight = self.n >> (p + 1)
            v = self.value(owner, h, p)
            u = u + weight * (v if t & weight else 1 - v)
        return h * self.half + u * self.m

    def base(self, h, t):
        return h * self.half + t * self.m

    def phase(self, t):
        p = 0
        while t >= self.n - (self.n >> (p + 1)):
            p += 1
        return p


def forward_kernel(
    plan, per_dev, pos_s, row_s, col_s, psf_s, scene, observed, weights, bank_h, psf_h, adj,
    near, bank, psf, obs, ivar, terms, got, load_sem, halo_send, halo_recv,
    rs_send, rs_recv, ag_send, ag_recv,
):
    n, m, c = plan.n, plan.m, plan.c
    kernels = bank_h.shape[0]
    owner = lax.axis_index("scene")
    strip = lax.axis_index("expo")
    strips = lax.axis_size("expo")

    barrier = pltpu.get_barrier_semaphore()
    for p in range(plan.bits):
        pl.semaphore_signal(
            barrier, inc=1, device_id={"scene": plan.partner(owner, 0, p)}, device_id_type=MESH
        )

    @pl.when(strip > 0)
    def _():
        pl.semaphore_signal(barrier, inc=1, device_id={"expo": strip - 1}, device_id_type=MESH)

    @pl.when(strip < strips - 1)
    def _():
        pl.semaphore_signal(barrier, inc=1, device_id={"expo": strip + 1}, device_id_type=MESH)

    loads = [
        pltpu.make_async_copy(scene, near.at[pl.ds(per_dev, per_dev)], load_sem.at[0]),
        pltpu.make_async_copy(bank_h, bank.at[pl.ds(0, kernels)], load_sem.at[1]),
        pltpu.make_async_copy(psf_h, psf, load_sem.at[2]),
    ]
    for h in range(2):
        home = plan.unit(owner, h, n - 1)
        loads.append(
            pltpu.make_async_copy(
                observed.at[pl.ds(home, m)], obs.at[pl.ds(h * m, m)], load_sem.at[3 + 2 * h]
            )
        )
        loads.append(
            pltpu.make_async_copy(
                weights.at[pl.ds(home, m)], ivar.at[pl.ds(h * m, m)], load_sem.at[4 + 2 * h]
            )
        )
    for load in loads:
        load.start()
    bank[kernels] = jnp.zeros(bank.shape[1:], bank.dtype)

    below = jnp.where(strip > 0, 1, 0)
    above = jnp.where(strip < strips - 1, 1, 0)
    pl.semaphore_wait(barrier, plan.bits + below + above)

    def halo(k, target):
        return pltpu.make_async_remote_copy(
            src_ref=scene,
            dst_ref=near.at[pl.ds(2 * k * per_dev, per_dev)],
            send_sem=halo_send.at[k],
            recv_sem=halo_recv.at[k],
            device_id={"expo": target},
            device_id_type=MESH,
        )

    @pl.when(strip < strips - 1)
    def _():
        halo(0, strip + 1).start()

    @pl.when(strip > 0)
    def _():
        halo(1, strip - 1).start()

    for load in loads:
        load.wait()

    @pl.when(strip > 0)
    def _():
        halo(0, strip).wait_recv()

    @pl.when(strip < strips - 1)
    def _():
        halo(1, strip).wait_recv()

    def scatter_copy(h, t, k):
        where = plan.base(h, t) + k * c
        slot = where // c
        return pltpu.make_async_remote_copy(
            src_ref=terms.at[pl.ds(where, c)],
            dst_ref=got.at[pl.ds(where, c)],
            send_sem=rs_send.at[slot],
            recv_sem=rs_recv.at[slot],
            device_id={"scene": plan.partner(owner, h, plan.phase(t))},
            device_id_type=MESH,
        )

    def gather_copy(h, t, p, k):
        source = plan.base(h, t) + k * c
        target = plan.base(h, t - (n >> (p + 1))) + k * c
        slot = target // c
        return pltpu.make_async_remote_copy(
            src_ref=adj.at[pl.ds(source, c)],
            dst_ref=adj.at[pl.ds(target, c)],
            send_sem=ag_send.at[slot],
            recv_sem=ag_recv.at[slot],
            device_id={"scene": plan.partner(owner, h, p)},
            device_id_type=MESH,
        )

    def make_terms(h, t, k):
        where = plan.base(h, t) + k * c
        first = plan.unit(owner, h, t) + k * c

        def body(i, carry):
            for e in range(UNROLL):
                j = first + i * UNROLL + e
                block = near[pos_s[j]]
                inner = dot(block, bank[col_s[j]], NT).astype(jnp.bfloat16)
                term = dot(bank[row_s[j]], inner, NN).astype(jnp.bfloat16)
                terms[where + i * UNROLL + e] = term
            return carry

        lax.fori_loop(0, c // UNROLL, body, 0)

    def arrived(t):
        return [t - (n >> (q + 1)) for q in range(plan.bits) if t >= n - (n >> (q + 1))]

    def summed(h, t, k, i):
        total = terms[plan.base(h, t) + k * c + i].astype(jnp.float32)
        for source in arrived(t):
            total = total + got[plan.base(h, source) + k * c + i].astype(jnp.float32)
        return total.astype(jnp.bfloat16)

    def pass_on(h, t, k):
        where = plan.base(h, t) + k * c

        def body(i, carry):
            terms[where + i] = summed(h, t, k, i)
            return carry

        lax.fori_loop(0, c, body, 0)

    def psf_pass(h, k):
        where = plan.base(h, n - 1) + k * c
        first = plan.unit(owner, h, n - 1) + k * c
        here = h * m + k * c

        def body(i, carry):
            for e in range(UNROLL):
                a = i * UNROLL + e
                q = psf[psf_s[first + a]]
                half = dot(summed(h, n - 1, k, a), q, NT).astype(jnp.bfloat16)
                model = dot(q, half, NN)
                weighted = (
                    ivar[here + a].astype(jnp.float32) * (model - obs[here + a].astype(jnp.float32))
                ).astype(jnp.bfloat16)
                back = dot(weighted, q, NN).astype(jnp.bfloat16)
                adj[where + a] = dot(q, back, TN).astype(jnp.bfloat16)
            return carry

        lax.fori_loop(0, c // UNROLL, body, 0)

    for t in range(n):
        for k in range(plan.chunks):
            for h in range(2):
                make_terms(h, t, k)
                if t < n // 2:
                    scatter_copy(h, t, k).start()
    for t in range(n // 2, n):
        for k in range(plan.chunks):
            for h in range(2):
                for source in arrived(t):
                    scatter_copy(h, source, k).wait_recv()
                if t < n - 1:
                    pass_on(h, t, k)
                    scatter_copy(h, t, k).start()
                else:
                    psf_pass(h, k)
                    for p in reversed(range(plan.bits)):
                        gather_copy(h, n - 1, p, k).start()
    for last in reversed(range(plan.bits)):
        for t in range(n - (n >> last), n - (n >> (last + 1))):
            for k in range(plan.chunks):
                for h in range(2):
                    gather_copy(h, t + (n >> (last + 1)), last, k).wait_recv()
                    for p in reversed(range(last)):
                        gather_copy(h, t, p, k).start()
    for t in range(n - 1):
        for k in range(plan.chunks):
            for h in range(2):
                scatter_copy(h, t, k).wait_send()
                p = plan.phase(t)
                gather_copy(h, t + (n >> (p + 1)), p, k).wait_send()

    @pl.when(strip < strips - 1)
    def _():
        halo(0, strip).wait_send()

    @pl.when(strip > 0)
    def _():
        halo(1, strip).wait_send()


def forward(plan, position, row, col, psf_index, scene, observed, weights, bank, psf):
    per_dev = scene.shape[0]
    blocks, side = position.shape[0], scene.shape[1:]
    slots = blocks // plan.c
    dtype = scene.dtype
    smem = pl.BlockSpec(memory_space=pltpu.SMEM)
    hbm = pl.BlockSpec(memory_space=pl.ANY)
    dma = pltpu.SemaphoreType.DMA
    return pl.pallas_call(
        functools.partial(forward_kernel, plan, per_dev),
        out_shape=jax.ShapeDtypeStruct((blocks, *side), dtype),
        in_specs=[smem] * 4 + [hbm] * 5,
        out_specs=pl.BlockSpec(memory_space=pltpu.VMEM),
        scratch_shapes=[
            pltpu.VMEM((3 * per_dev, *side), dtype),
            pltpu.VMEM((bank.shape[0] + 1, *side), dtype),
            pltpu.VMEM(psf.shape, dtype),
            pltpu.VMEM((2 * plan.m, *side), dtype),
            pltpu.VMEM((2 * plan.m, *side), dtype),
            pltpu.VMEM((blocks, *side), dtype),
            pltpu.VMEM((blocks, *side), dtype),
            dma((7,)),
            dma((2,)),
            dma((2,)),
            dma((slots,)),
            dma((slots,)),
            dma((slots,)),
            dma((slots,)),
        ],
        compiler_params=pltpu.CompilerParams(
            collective_id=0, has_side_effects=True, vmem_limit_bytes=VMEM_LIMIT
        ),
        name="forward",
    )(position, row, col, psf_index, scene, observed, weights, bank, psf)


def backward_kernel(
    plan, per_dev, outer, pos_s, row_s, col_s, adj, bank_h, *rest
):
    if outer:
        lower, upper, total, bank, lists, sem = rest
    else:
        total, bank, lists, sem = rest
    kernels = bank_h.shape[0]
    load = pltpu.make_async_copy(bank_h, bank.at[pl.ds(0, kernels)], sem)
    load.start()
    bank[kernels] = jnp.zeros(bank.shape[1:], bank.dtype)

    def clear(i, carry):
        total[i] = jnp.zeros(total.shape[1:], total.dtype)
        return carry

    lax.fori_loop(0, total.shape[0], clear, 0, unroll=2)
    owner = lax.axis_index("scene")
    count = 0
    for h in range(2):
        for t in range(plan.n):
            first, base = plan.unit(owner, h, t), plan.base(h, t)

            def pick(i, count, first=first, base=base):
                position = pos_s[first + i]
                row = row_s[first + i]
                inside = jnp.logical_and(position >= per_dev, position < 2 * per_dev)
                if outer:
                    wanted = jnp.logical_and(row < kernels, jnp.logical_not(inside))
                    slot = jnp.where(position < per_dev, position, position - per_dev)
                else:
                    wanted = jnp.logical_and(row < kernels, inside)
                    slot = position - per_dev
                lists[0, count] = slot
                lists[1, count] = row
                lists[2, count] = col_s[first + i]
                lists[3, count] = base + i
                return count + wanted.astype(jnp.int32)

            count = lax.fori_loop(0, plan.m, pick, count)
    for e in range(UNROLL):
        lists[0, count + e] = 0
        lists[1, count + e] = kernels
        lists[2, count + e] = 0
        lists[3, count + e] = 0
    load.wait()

    def body(i, carry):
        pulled = []
        for e in range(UNROLL):
            a = i * UNROLL + e
            spread = dot(adj[lists[3, a]], bank[lists[2, a]], NN).astype(jnp.bfloat16)
            pulled.append(dot(bank[lists[1, a]], spread, TN))
        for e in range(UNROLL):
            slot = lists[0, i * UNROLL + e]
            total[slot] = total[slot] + pulled[e]
        return carry

    lax.fori_loop(0, (count + UNROLL - 1) // UNROLL, body, 0)
    if outer:

        def put(i, carry):
            lower[i] = total[i].astype(lower.dtype)
            upper[i] = total[per_dev + i].astype(upper.dtype)
            return carry

        lax.fori_loop(0, per_dev, put, 0)


def backward(plan, outer, per_dev, position, row, col, adj, bank):
    side = adj.shape[1:]
    smem = pl.BlockSpec(memory_space=pltpu.SMEM)
    vmem = pl.BlockSpec(memory_space=pltpu.VMEM)
    scratch = [
        pltpu.VMEM((bank.shape[0] + 1, *side), bank.dtype),
        pltpu.SMEM((4, adj.shape[0] + UNROLL), jnp.int32),
        pltpu.SemaphoreType.DMA,
    ]
    if outer:
        shape = [jax.ShapeDtypeStruct((per_dev, *side), jnp.bfloat16)] * 2
        scratch = [pltpu.VMEM((2 * per_dev, *side), jnp.float32)] + scratch
    else:
        shape = jax.ShapeDtypeStruct((per_dev, *side), jnp.float32)
    return pl.pallas_call(
        functools.partial(backward_kernel, plan, per_dev, outer),
        out_shape=shape,
        in_specs=[smem] * 3 + [vmem, pl.BlockSpec(memory_space=pl.ANY)],
        out_specs=[vmem] * 2 if outer else vmem,
        scratch_shapes=scratch,
        compiler_params=pltpu.CompilerParams(vmem_limit_bytes=VMEM_LIMIT // 2),
        cost_estimate=pl.CostEstimate(
            flops=4 * side[0] ** 3 * adj.shape[0] * 4,
            bytes_accessed=adj.size * 4,
            transcendentals=0,
        ),
        name="outer" if outer else "inner",
    )(position, row, col, adj, bank)


def on_device(
    scene,
    observed,
    inverse_variance,
    intersection,
    resample_index,
    psf_index,
    resample_bank,
    psf_bank,
):
    owner = lax.axis_index("scene")
    strips = lax.axis_size("expo")
    strip = lax.axis_index("expo")
    per_dev = scene.shape[0]
    width = intersection.shape[1]
    kernels = resample_bank.shape[0]
    plan = Plan(lax.axis_size("scene"), intersection.shape[0])
    match = intersection // (strips * per_dev) == owner
    live = jnp.any(match, axis=1)
    place = (intersection // per_dev % strips - strip + 1) * per_dev + intersection % per_dev
    place = jnp.clip(place, 0, 3 * per_dev - 1)
    position = jnp.where(live, jnp.sum(jnp.where(match, place, 0), axis=1), per_dev)
    row = jnp.sum(jnp.where(match, resample_index[:, :width], 0), axis=1)
    row = jnp.where(live, row, kernels)
    col = jnp.sum(jnp.where(match, resample_index[:, width:], 0), axis=1)
    adj = forward(
        plan, position, row, col, psf_index, scene, observed, inverse_variance, resample_bank,
        psf_bank,
    )
    lower, upper = backward(plan, True, per_dev, position, row, col, adj, resample_bank)
    from_above = passed_along(lower, "expo", -1)
    from_below = passed_along(upper, "expo", 1)
    middle = backward(plan, False, per_dev, position, row, col, adj, resample_bank)
    return middle + from_above.astype(jnp.float32) + from_below.astype(jnp.float32)


def solution(mesh):
    return jax.shard_map(
        on_device,
        mesh=mesh,
        in_specs=(
            P(("scene", "expo"), None, None),
            P("expo", None, None),
            P("expo", None, None),
            P("expo", None),
            P("expo", None),
            P("expo"),
            P(),
            P(),
        ),
        out_specs=P(("scene", "expo"), None, None),
        check_vma=False,
    )
```

```python
import functools

import jax
import jax.numpy as jnp
from jax import lax
from jax.experimental import pallas as pl
from jax.experimental.pallas import tpu as pltpu
from jax.sharding import PartitionSpec as P

MESH = pl.DeviceIdType.MESH
UNROLL = 4
PIECES = 4
VMEM_LIMIT = 60 * 1024 * 1024


def dot(a, b, dims):
    return lax.dot_general(a, b, (dims, ((), ())), preferred_element_type=jnp.float32)


NN = ((1,), (0,))
NT = ((1,), (1,))
TN = ((0,), (0,))


class Plan:
    def __init__(self, owners, exposures):
        self.n = owners
        self.bits = owners.bit_length() - 1
        assert 1 << self.bits == owners
        self.half = exposures // 2
        self.m = self.half // owners
        self.c = min(8, self.m)
        self.chunks = self.m // self.c

    def bit(self, h, p):
        return p if h == 0 else self.bits - 1 - p

    def value(self, owner, h, p):
        return (owner // (1 << self.bit(h, p))) % 2

    def partner(self, owner, h, p):
        step = 1 << self.bit(h, p)
        return owner + step - 2 * step * self.value(owner, h, p)

    def unit(self, owner, h, t):
        u = 0
        for p in range(self.bits):
            weight = self.n >> (p + 1)
            v = self.value(owner, h, p)
            u = u + weight * (v if t & weight else 1 - v)
        return h * self.half + u * self.m

    def base(self, h, t):
        return h * self.half + t * self.m

    def turn(self, h, t, k):
        return (((self.n - 1 - t) * self.chunks + k) * 2 + h) * self.c

    def turns(self, owner, exposures):
        j = jnp.arange(exposures, dtype=jnp.int32)
        h, u, i = j // self.half, j % self.half // self.m, j % self.m
        me = [self.unit(owner, h, self.n - 1) - h * self.half for h in range(2)]
        apart = jnp.bitwise_xor(u, jnp.where(h == 0, me[0], me[1]) // self.m)
        return ((apart * self.chunks + i // self.c) * 2 + h) * self.c + i % self.c

    def phase(self, t):
        p = 0
        while t >= self.n - (self.n >> (p + 1)):
            p += 1
        return p


def forward_kernel(
    plan, per_dev, pos_s, row_s, col_s, psf_s, prev_s, last_s, scene, observed, weights, bank_h,
    psf_h, middle_h, above_h, below_h,
    near, bank, psf, obs, ivar, terms, got, adj, run, edge, middle, load_sem, halo_send, halo_recv,
    rs_send, rs_recv, ag_send, ag_recv, lower_send, lower_recv, upper_send, upper_recv, store_sem,
):
    n, m, c = plan.n, plan.m, plan.c
    kernels = bank_h.shape[0]
    owner = lax.axis_index("scene")
    strip = lax.axis_index("expo")
    strips = lax.axis_size("expo")

    barrier = pltpu.get_barrier_semaphore()
    for p in range(plan.bits):
        pl.semaphore_signal(
            barrier, inc=1, device_id={"scene": plan.partner(owner, 0, p)}, device_id_type=MESH
        )

    @pl.when(strip > 0)
    def _():
        pl.semaphore_signal(barrier, inc=1, device_id={"expo": strip - 1}, device_id_type=MESH)

    @pl.when(strip < strips - 1)
    def _():
        pl.semaphore_signal(barrier, inc=1, device_id={"expo": strip + 1}, device_id_type=MESH)

    loads = [
        pltpu.make_async_copy(scene, near.at[pl.ds(per_dev, per_dev)], load_sem.at[0]),
        pltpu.make_async_copy(bank_h, bank.at[pl.ds(0, kernels)], load_sem.at[1]),
        pltpu.make_async_copy(psf_h, psf, load_sem.at[2]),
    ]
    for h in range(2):
        home = plan.unit(owner, h, n - 1)
        loads.append(
            pltpu.make_async_copy(
                observed.at[pl.ds(home, m)], obs.at[pl.ds(h * m, m)], load_sem.at[3 + 2 * h]
            )
        )
        loads.append(
            pltpu.make_async_copy(
                weights.at[pl.ds(home, m)], ivar.at[pl.ds(h * m, m)], load_sem.at[4 + 2 * h]
            )
        )
    for load in loads:
        load.start()
    bank[kernels] = jnp.zeros(bank.shape[1:], bank.dtype)
    run[0] = jnp.zeros(run.shape[1:], run.dtype)

    below = jnp.where(strip > 0, 1, 0)
    above = jnp.where(strip < strips - 1, 1, 0)
    pl.semaphore_wait(barrier, plan.bits + below + above)

    def halo(k, target):
        return pltpu.make_async_remote_copy(
            src_ref=scene,
            dst_ref=near.at[pl.ds(2 * k * per_dev, per_dev)],
            send_sem=halo_send.at[k],
            recv_sem=halo_recv.at[k],
            device_id={"expo": target},
            device_id_type=MESH,
        )

    @pl.when(strip < strips - 1)
    def _():
        halo(0, strip + 1).start()

    @pl.when(strip > 0)
    def _():
        halo(1, strip - 1).start()

    for load in loads:
        load.wait()

    @pl.when(strip > 0)
    def _():
        halo(0, strip).wait_recv()

    @pl.when(strip < strips - 1)
    def _():
        halo(1, strip).wait_recv()

    def scatter_copy(h, t, k):
        where = plan.base(h, t) + k * c
        slot = where // c
        return pltpu.make_async_remote_copy(
            src_ref=terms.at[pl.ds(where, c)],
            dst_ref=got.at[pl.ds(where, c)],
            send_sem=rs_send.at[slot],
            recv_sem=rs_recv.at[slot],
            device_id={"scene": plan.partner(owner, h, plan.phase(t))},
            device_id_type=MESH,
        )

    def gather_copy(h, t, p, k):
        source = plan.base(h, t) + k * c
        target = plan.base(h, t - (n >> (p + 1))) + k * c
        slot = target // c
        return pltpu.make_async_remote_copy(
            src_ref=adj.at[pl.ds(source, c)],
            dst_ref=adj.at[pl.ds(target, c)],
            send_sem=ag_send.at[slot],
            recv_sem=ag_recv.at[slot],
            device_id={"scene": plan.partner(owner, h, p)},
            device_id_type=MESH,
        )

    def make_terms(h, t, k):
        where = plan.base(h, t) + k * c
        first = plan.unit(owner, h, t) + k * c

        def body(i, carry):
            for e in range(UNROLL):
                j = first + i * UNROLL + e
                block = near[pos_s[j]]
                inner = dot(block, bank[col_s[j]], NT).astype(jnp.bfloat16)
                term = dot(bank[row_s[j]], inner, NN).astype(jnp.bfloat16)
                terms[where + i * UNROLL + e] = term
            return carry

        lax.fori_loop(0, c // UNROLL, body, 0)

    def arrived(t):
        return [t - (n >> (q + 1)) for q in range(plan.bits) if t >= n - (n >> (q + 1))]

    def summed(h, t, k, i):
        total = terms[plan.base(h, t) + k * c + i].astype(jnp.float32)
        for source in arrived(t):
            total = total + got[plan.base(h, source) + k * c + i].astype(jnp.float32)
        return total.astype(jnp.bfloat16)

    def pass_on(h, t, k):
        where = plan.base(h, t) + k * c

        def body(i, carry):
            terms[where + i] = summed(h, t, k, i)
            return carry

        lax.fori_loop(0, c, body, 0)

    def psf_pass(h, k):
        where = plan.base(h, n - 1) + k * c
        first = plan.unit(owner, h, n - 1) + k * c
        here = h * m + k * c

        def body(i, carry):
            for e in range(UNROLL):
                a = i * UNROLL + e
                q = psf[psf_s[first + a]]
                half = dot(summed(h, n - 1, k, a), q, NT).astype(jnp.bfloat16)
                model = dot(q, half, NN)
                weighted = (
                    ivar[here + a].astype(jnp.float32) * (model - obs[here + a].astype(jnp.float32))
                ).astype(jnp.bfloat16)
                back = dot(weighted, q, NN).astype(jnp.bfloat16)
                adj[where + a] = dot(q, back, TN).astype(jnp.bfloat16)
            return carry

        lax.fori_loop(0, c // UNROLL, body, 0)

    for t in range(n):
        for k in range(plan.chunks):
            for h in range(2):
                make_terms(h, t, k)
                if t < n // 2:
                    scatter_copy(h, t, k).start()
    for t in range(n // 2, n):
        for k in range(plan.chunks):
            for h in range(2):
                for source in arrived(t):
                    scatter_copy(h, source, k).wait_recv()
                if t < n - 1:
                    pass_on(h, t, k)
                    scatter_copy(h, t, k).start()
                else:
                    psf_pass(h, k)
                    for p in reversed(range(plan.bits)):
                        gather_copy(h, n - 1, p, k).start()
    def pull(h, t, k):
        where = plan.base(h, t) + k * c
        first = plan.unit(owner, h, t) + k * c
        place = 1 + plan.turn(h, t, k)

        def body(i, carry):
            pulled = []
            for e in range(UNROLL):
                j = first + i * UNROLL + e
                spread = dot(adj[where + i * UNROLL + e], bank[col_s[j]], NN).astype(jnp.bfloat16)
                pulled.append(dot(bank[row_s[j]], spread, TN))
            for e in range(UNROLL):
                j = first + i * UNROLL + e
                run[place + i * UNROLL + e] = pulled[e] + run[prev_s[j]]
            return carry

        lax.fori_loop(0, c // UNROLL, body, 0)

    for k in range(plan.chunks):
        for h in range(2):
            pull(h, n - 1, k)
    for last in reversed(range(plan.bits)):
        for t in reversed(range(n - (n >> last), n - (n >> (last + 1)))):
            for k in range(plan.chunks):
                for h in range(2):
                    gather_copy(h, t + (n >> (last + 1)), last, k).wait_recv()
                    for p in reversed(range(last)):
                        gather_copy(h, t, p, k).start()
                    pull(h, t, k)

    def edge_copy(up, piece):
        out, send, recv = (
            (below_h, upper_send, upper_recv) if up else (above_h, lower_send, lower_recv)
        )
        return pltpu.make_async_remote_copy(
            src_ref=edge.at[pl.ds(up * per_dev + piece * size, size)],
            dst_ref=out.at[pl.ds(piece * size, size)],
            send_sem=send.at[piece],
            recv_sem=recv.at[piece],
            device_id={"expo": strip + (1 if up else -1)},
            device_id_type=MESH,
        )

    pieces = lower_send.shape[0]
    size = per_dev // pieces
    for piece in range(pieces):
        for up in range(2):

            def put(i, carry, up=up, piece=piece):
                a = piece * size + i
                edge[up * per_dev + a] = run[last_s[2 * up * per_dev + a]].astype(edge.dtype)
                return carry

            lax.fori_loop(0, size, put, 0, unroll=2)

            @pl.when(strip < strips - 1 if up else strip > 0)
            def _(up=up, piece=piece):
                edge_copy(up, piece).start()

    def own(i, carry):
        middle[i] = run[last_s[per_dev + i]]
        return carry

    lax.fori_loop(0, per_dev, own, 0, unroll=2)
    store = pltpu.make_async_copy(middle, middle_h, store_sem)
    store.start()

    for t in range(n - 1):
        for k in range(plan.chunks):
            for h in range(2):
                scatter_copy(h, t, k).wait_send()
                p = plan.phase(t)
                gather_copy(h, t + (n >> (p + 1)), p, k).wait_send()

    @pl.when(strip < strips - 1)
    def _():
        halo(0, strip).wait_send()
        for piece in range(pieces):
            edge_copy(1, piece).wait_send()
            edge_copy(0, piece).wait_recv()

    @pl.when(strip > 0)
    def _():
        halo(1, strip).wait_send()
        for piece in range(pieces):
            edge_copy(0, piece).wait_send()
            edge_copy(1, piece).wait_recv()

    store.wait()


def gradient_parts(plan, tables, scene, observed, weights, bank, psf):
    per_dev = scene.shape[0]
    blocks, side = tables[0].shape[0], scene.shape[1:]
    slots = blocks // plan.c
    pieces = PIECES
    dtype = scene.dtype
    smem = pl.BlockSpec(memory_space=pltpu.SMEM)
    hbm = pl.BlockSpec(memory_space=pl.ANY)
    dma = pltpu.SemaphoreType.DMA
    return pl.pallas_call(
        functools.partial(forward_kernel, plan, per_dev),
        out_shape=[
            jax.ShapeDtypeStruct((per_dev, *side), jnp.float32),
            jax.ShapeDtypeStruct((per_dev, *side), jnp.bfloat16),
            jax.ShapeDtypeStruct((per_dev, *side), jnp.bfloat16),
        ],
        in_specs=[smem] * len(tables) + [hbm] * 5,
        out_specs=[hbm] * 3,
        scratch_shapes=[
            pltpu.VMEM((3 * per_dev, *side), dtype),
            pltpu.VMEM((bank.shape[0] + 1, *side), dtype),
            pltpu.VMEM(psf.shape, dtype),
            pltpu.VMEM((2 * plan.m, *side), dtype),
            pltpu.VMEM((2 * plan.m, *side), dtype),
            pltpu.VMEM((blocks, *side), dtype),
            pltpu.VMEM((blocks, *side), dtype),
            pltpu.VMEM((blocks, *side), dtype),
            pltpu.VMEM((blocks + 1, *side), jnp.float32),
            pltpu.VMEM((2 * per_dev, *side), jnp.bfloat16),
            pltpu.VMEM((per_dev, *side), jnp.float32),
            dma((7,)),
            dma((2,)),
            dma((2,)),
            dma((slots,)),
            dma((slots,)),
            dma((slots,)),
            dma((slots,)),
            dma((pieces,)),
            dma((pieces,)),
            dma((pieces,)),
            dma((pieces,)),
            dma,
        ],
        compiler_params=pltpu.CompilerParams(
            collective_id=0, has_side_effects=True, vmem_limit_bytes=VMEM_LIMIT
        ),
        name="gradient",
    )(*tables, scene, observed, weights, bank, psf)


def on_device(
    scene,
    observed,
    inverse_variance,
    intersection,
    resample_index,
    psf_index,
    resample_bank,
    psf_bank,
):
    owner = lax.axis_index("scene")
    strips = lax.axis_size("expo")
    strip = lax.axis_index("expo")
    per_dev = scene.shape[0]
    width = intersection.shape[1]
    kernels = resample_bank.shape[0]
    plan = Plan(lax.axis_size("scene"), intersection.shape[0])
    match = intersection // (strips * per_dev) == owner
    live = jnp.any(match, axis=1)
    place = (intersection // per_dev % strips - strip + 1) * per_dev + intersection % per_dev
    place = jnp.clip(place, 0, 3 * per_dev - 1)
    position = jnp.where(live, jnp.sum(jnp.where(match, place, 0), axis=1), per_dev)
    row = jnp.sum(jnp.where(match, resample_index[:, :width], 0), axis=1)
    row = jnp.where(live, row, kernels)
    col = jnp.sum(jnp.where(match, resample_index[:, width:], 0), axis=1)
    slot = jnp.where(live, position, -1)
    turn = plan.turns(owner, slot.shape[0])
    before = (slot[:, None] == slot[None, :]) & (turn[None, :] < turn[:, None])
    prev = jnp.max(jnp.where(before, turn[None, :] + 1, 0), axis=1)
    slots = jnp.arange(3 * per_dev, dtype=jnp.int32)
    last = jnp.max(jnp.where(slots[:, None] == slot[None, :], turn[None, :] + 1, 0), axis=1)
    middle, above, below = gradient_parts(
        plan, (position, row, col, psf_index, prev, last), scene, observed, inverse_variance,
        resample_bank, psf_bank,
    )
    above = jnp.where(strip < strips - 1, above.astype(jnp.float32), 0.0)
    below = jnp.where(strip > 0, below.astype(jnp.float32), 0.0)
    return middle + above + below


def solution(mesh):
    return jax.shard_map(
        on_device,
        mesh=mesh,
        in_specs=(
            P(("scene", "expo"), None, None),
            P("expo", None, None),
            P("expo", None, None),
            P("expo", None),
            P("expo", None),
            P("expo"),
            P(),
            P(),
        ),
        out_specs=P(("scene", "expo"), None, None),
        check_vma=False,
    )
```

```python
import functools

import jax
import jax.numpy as jnp
from jax import lax
from jax.experimental import pallas as pl
from jax.experimental.pallas import tpu as pltpu
from jax.sharding import PartitionSpec as P

MESH = pl.DeviceIdType.MESH
UNROLL = 4
PIECES = 4
VMEM_LIMIT = 50 * 1024 * 1024


def dot(a, b, dims):
    return lax.dot_general(a, b, (dims, ((), ())), preferred_element_type=jnp.float32)


NN = ((1,), (0,))
NT = ((1,), (1,))
TN = ((0,), (0,))


def passed_along(value, axis, steps):
    count = lax.axis_size(axis)
    initial, last = (max(0, -steps), min(count, count - steps))
    return lax.ppermute(value, axis, [(source, source + steps) for source in range(initial, last)])


class Plan:
    def __init__(self, owners, exposures):
        self.n = owners
        self.bits = owners.bit_length() - 1
        assert 1 << self.bits == owners
        self.half = exposures // 2
        self.m = self.half // owners
        self.c = min(8, self.m)
        self.chunks = self.m // self.c

    def bit(self, h, p):
        return p if h == 0 else self.bits - 1 - p

    def value(self, owner, h, p):
        return (owner // (1 << self.bit(h, p))) % 2

    def partner(self, owner, h, p):
        step = 1 << self.bit(h, p)
        return owner + step - 2 * step * self.value(owner, h, p)

    def unit(self, owner, h, t):
        u = 0
        for p in range(self.bits):
            weight = self.n >> (p + 1)
            v = self.value(owner, h, p)
            u = u + weight * (v if t & weight else 1 - v)
        return h * self.half + u * self.m

    def base(self, h, t):
        return h * self.half + t * self.m

    def turn(self, h, t, k):
        return (((self.n - 1 - t) * self.chunks + k) * 2 + h) * self.c

    def turns(self, owner, exposures):
        j = jnp.arange(exposures, dtype=jnp.int32)
        h, u, i = j // self.half, j % self.half // self.m, j % self.m
        me = [self.unit(owner, h, self.n - 1) - h * self.half for h in range(2)]
        apart = jnp.bitwise_xor(u, jnp.where(h == 0, me[0], me[1]) // self.m)
        return ((apart * self.chunks + i // self.c) * 2 + h) * self.c + i % self.c

    def phase(self, t):
        p = 0
        while t >= self.n - (self.n >> (p + 1)):
            p += 1
        return p


def forward_kernel(
    plan, per_dev, pos_s, own_s, give_s, row_s, col_s, psf_s, prev_s, last_s, scene, observed, weights, bank_h,
    psf_h, middle_h, above_h, below_h,
    held, stage, came, bank, psf, obs, ivar, terms, got, adj, run, middle, load_sem, z_send, z_recv,
    rs_send, rs_recv, ag_send, ag_recv, lower_send, lower_recv, upper_send, upper_recv, store_sem,
):
    n, m, c = plan.n, plan.m, plan.c
    kernels = bank_h.shape[0]
    owner = lax.axis_index("scene")
    strip = lax.axis_index("expo")
    strips = lax.axis_size("expo")

    barrier = pltpu.get_barrier_semaphore()
    for p in range(plan.bits):
        pl.semaphore_signal(
            barrier, inc=1, device_id={"scene": plan.partner(owner, 0, p)}, device_id_type=MESH
        )

    @pl.when(strip > 0)
    def _():
        pl.semaphore_signal(barrier, inc=1, device_id={"expo": strip - 1}, device_id_type=MESH)

    @pl.when(strip < strips - 1)
    def _():
        pl.semaphore_signal(barrier, inc=1, device_id={"expo": strip + 1}, device_id_type=MESH)

    loads = [
        pltpu.make_async_copy(scene, held, load_sem.at[0]),
        pltpu.make_async_copy(bank_h, bank.at[pl.ds(0, kernels)], load_sem.at[1]),
        pltpu.make_async_copy(psf_h, psf, load_sem.at[2]),
    ]
    for h in range(2):
        home = plan.unit(owner, h, n - 1)
        loads.append(
            pltpu.make_async_copy(
                observed.at[pl.ds(home, m)], obs.at[pl.ds(h * m, m)], load_sem.at[3 + 2 * h]
            )
        )
        loads.append(
            pltpu.make_async_copy(
                weights.at[pl.ds(home, m)], ivar.at[pl.ds(h * m, m)], load_sem.at[4 + 2 * h]
            )
        )
    for load in loads:
        load.start()
    bank[kernels] = jnp.zeros(bank.shape[1:], bank.dtype)
    run[0] = jnp.zeros(run.shape[1:], run.dtype)

    below = jnp.where(strip > 0, 1, 0)
    above = jnp.where(strip < strips - 1, 1, 0)
    pl.semaphore_wait(barrier, plan.bits + below + above)

    blocks = terms.shape[0]

    def z_copy(up, h, t, k):
        where = (0 if up else blocks) + plan.base(h, t) + k * c
        return pltpu.make_async_remote_copy(
            src_ref=stage.at[pl.ds(where, c)],
            dst_ref=came.at[pl.ds(where, c)],
            send_sem=z_send.at[where // c],
            recv_sem=z_recv.at[where // c],
            device_id={"expo": strip + (1 if up else -1)},
            device_id_type=MESH,
        )

    loads[0].wait()
    for t in range(n):
        for k in range(plan.chunks):
            for h in range(2):
                for up in (1, 0):
                    first = (0 if up else blocks) + plan.unit(owner, h, t) + k * c
                    where = (0 if up else blocks) + plan.base(h, t) + k * c

                    def fill(i, carry, first=first, where=where):
                        stage[where + i] = held[give_s[first + i]]
                        return carry

                    lax.fori_loop(0, c, fill, 0, unroll=2)

                    @pl.when(strip < strips - 1 if up else strip > 0)
                    def _(up=up, h=h, t=t, k=k):
                        z_copy(up, h, t, k).start()

    @pl.when(strip == 0)
    def _():
        def wipe(i, carry):
            came[i] = jnp.zeros(came.shape[1:], came.dtype)
            return carry

        lax.fori_loop(0, blocks, wipe, 0)

    @pl.when(strip == strips - 1)
    def _():
        def wipe(i, carry):
            came[blocks + i] = jnp.zeros(came.shape[1:], came.dtype)
            return carry

        lax.fori_loop(0, blocks, wipe, 0)

    for load in loads[1:]:
        load.wait()

    def scatter_copy(h, t, k):
        where = plan.base(h, t) + k * c
        slot = where // c
        return pltpu.make_async_remote_copy(
            src_ref=terms.at[pl.ds(where, c)],
            dst_ref=got.at[pl.ds(where, c)],
            send_sem=rs_send.at[slot],
            recv_sem=rs_recv.at[slot],
            device_id={"scene": plan.partner(owner, h, plan.phase(t))},
            device_id_type=MESH,
        )

    def gather_copy(h, t, p, k):
        source = plan.base(h, t) + k * c
        target = plan.base(h, t - (n >> (p + 1))) + k * c
        slot = target // c
        return pltpu.make_async_remote_copy(
            src_ref=adj.at[pl.ds(source, c)],
            dst_ref=adj.at[pl.ds(target, c)],
            send_sem=ag_send.at[slot],
            recv_sem=ag_recv.at[slot],
            device_id={"scene": plan.partner(owner, h, p)},
            device_id_type=MESH,
        )

    def make_terms(h, t, k):
        where = plan.base(h, t) + k * c
        first = plan.unit(owner, h, t) + k * c

        def body(i, carry):
            for e in range(UNROLL):
                j = first + i * UNROLL + e
                position = pos_s[j]
                here = where + i * UNROLL + e
                block = lax.select(position < per_dev, came[here], held[own_s[j]])
                block = lax.select(position >= 2 * per_dev, came[blocks + here], block)
                inner = dot(block, bank[col_s[j]], NT).astype(jnp.bfloat16)
                term = dot(bank[row_s[j]], inner, NN).astype(jnp.bfloat16)
                terms[where + i * UNROLL + e] = term
            return carry

        lax.fori_loop(0, c // UNROLL, body, 0)

    def arrived(t):
        return [t - (n >> (q + 1)) for q in range(plan.bits) if t >= n - (n >> (q + 1))]

    def summed(h, t, k, i):
        total = terms[plan.base(h, t) + k * c + i].astype(jnp.float32)
        for source in arrived(t):
            total = total + got[plan.base(h, source) + k * c + i].astype(jnp.float32)
        return total.astype(jnp.bfloat16)

    def pass_on(h, t, k):
        where = plan.base(h, t) + k * c

        def body(i, carry):
            terms[where + i] = summed(h, t, k, i)
            return carry

        lax.fori_loop(0, c, body, 0)

    def psf_pass(h, k):
        where = plan.base(h, n - 1) + k * c
        first = plan.unit(owner, h, n - 1) + k * c
        here = h * m + k * c

        def body(i, carry):
            for e in range(UNROLL):
                a = i * UNROLL + e
                q = psf[psf_s[first + a]]
                half = dot(summed(h, n - 1, k, a), q, NT).astype(jnp.bfloat16)
                model = dot(q, half, NN)
                weighted = (
                    ivar[here + a].astype(jnp.float32) * (model - obs[here + a].astype(jnp.float32))
                ).astype(jnp.bfloat16)
                back = dot(weighted, q, NN).astype(jnp.bfloat16)
                adj[where + a] = dot(q, back, TN).astype(jnp.bfloat16)
            return carry

        lax.fori_loop(0, c // UNROLL, body, 0)

    for t in range(n):
        for k in range(plan.chunks):
            for h in range(2):

                @pl.when(strip > 0)
                def _(h=h, t=t, k=k):
                    z_copy(1, h, t, k).wait_recv()

                @pl.when(strip < strips - 1)
                def _(h=h, t=t, k=k):
                    z_copy(0, h, t, k).wait_recv()

                make_terms(h, t, k)
                for source in arrived(t):
                    scatter_copy(h, source, k).wait_recv()
                if t < n // 2:
                    scatter_copy(h, t, k).start()
                elif t < n - 1:
                    pass_on(h, t, k)
                    scatter_copy(h, t, k).start()
                else:
                    psf_pass(h, k)
                    for p in reversed(range(plan.bits)):
                        gather_copy(h, n - 1, p, k).start()

    for t in range(n):
        for k in range(plan.chunks):
            for h in range(2):

                @pl.when(strip < strips - 1)
                def _(h=h, t=t, k=k):
                    z_copy(1, h, t, k).wait_send()

                @pl.when(strip > 0)
                def _(h=h, t=t, k=k):
                    z_copy(0, h, t, k).wait_send()

    def pull(h, t, k):
        where = plan.base(h, t) + k * c
        first = plan.unit(owner, h, t) + k * c
        place = 1 + plan.turn(h, t, k)

        def body(i, carry):
            pulled = []
            for e in range(UNROLL):
                j = first + i * UNROLL + e
                spread = dot(adj[where + i * UNROLL + e], bank[col_s[j]], NN).astype(jnp.bfloat16)
                pulled.append(dot(bank[row_s[j]], spread, TN))
            for e in range(UNROLL):
                j = first + i * UNROLL + e
                run[place + i * UNROLL + e] = pulled[e] + run[prev_s[j]]
            return carry

        lax.fori_loop(0, c // UNROLL, body, 0)

    for k in range(plan.chunks):
        for h in range(2):
            pull(h, n - 1, k)
    for last in reversed(range(plan.bits)):
        for t in reversed(range(n - (n >> last), n - (n >> (last + 1)))):
            for k in range(plan.chunks):
                for h in range(2):
                    gather_copy(h, t + (n >> (last + 1)), last, k).wait_recv()
                    for p in reversed(range(last)):
                        gather_copy(h, t, p, k).start()
                    pull(h, t, k)

    def edge_copy(up, piece):
        out, send, recv = (
            (below_h, upper_send, upper_recv) if up else (above_h, lower_send, lower_recv)
        )
        return pltpu.make_async_remote_copy(
            src_ref=stage.at[pl.ds(up * per_dev + piece * size, size)],
            dst_ref=out.at[pl.ds(piece * size, size)],
            send_sem=send.at[piece],
            recv_sem=recv.at[piece],
            device_id={"expo": strip + (1 if up else -1)},
            device_id_type=MESH,
        )

    pieces = lower_send.shape[0]
    size = per_dev // pieces
    for piece in range(pieces):
        for up in range(2):

            def put(i, carry, up=up, piece=piece):
                a = piece * size + i
                stage[up * per_dev + a] = run[last_s[2 * up * per_dev + a]].astype(stage.dtype)
                return carry

            lax.fori_loop(0, size, put, 0, unroll=2)

            @pl.when(strip < strips - 1 if up else strip > 0)
            def _(up=up, piece=piece):
                edge_copy(up, piece).start()

    def own(i, carry):
        middle[i] = run[last_s[per_dev + i]]
        return carry

    lax.fori_loop(0, per_dev, own, 0, unroll=2)
    store = pltpu.make_async_copy(middle, middle_h, store_sem)
    store.start()

    for t in range(n - 1):
        for k in range(plan.chunks):
            for h in range(2):
                scatter_copy(h, t, k).wait_send()
                p = plan.phase(t)
                gather_copy(h, t + (n >> (p + 1)), p, k).wait_send()

    @pl.when(strip < strips - 1)
    def _():
        for piece in range(pieces):
            edge_copy(1, piece).wait_send()
            edge_copy(0, piece).wait_recv()

    @pl.when(strip > 0)
    def _():
        for piece in range(pieces):
            edge_copy(0, piece).wait_send()
            edge_copy(1, piece).wait_recv()

    store.wait()


def gradient_parts(plan, tables, scene, observed, weights, bank, psf):
    per_dev = scene.shape[0]
    blocks, side = tables[0].shape[0], scene.shape[1:]
    slots = blocks // plan.c
    pieces = PIECES
    dtype = scene.dtype
    smem = pl.BlockSpec(memory_space=pltpu.SMEM)
    hbm = pl.BlockSpec(memory_space=pl.ANY)
    dma = pltpu.SemaphoreType.DMA
    return pl.pallas_call(
        functools.partial(forward_kernel, plan, per_dev),
        out_shape=[
            jax.ShapeDtypeStruct((per_dev, *side), jnp.float32),
            jax.ShapeDtypeStruct((per_dev, *side), jnp.bfloat16),
            jax.ShapeDtypeStruct((per_dev, *side), jnp.bfloat16),
        ],
        in_specs=[smem] * len(tables) + [hbm] * 5,
        out_specs=[hbm] * 3,
        scratch_shapes=[
            pltpu.VMEM((per_dev, *side), dtype),
            pltpu.VMEM((2 * blocks, *side), dtype),
            pltpu.VMEM((2 * blocks, *side), dtype),
            pltpu.VMEM((bank.shape[0] + 1, *side), dtype),
            pltpu.VMEM(psf.shape, dtype),
            pltpu.VMEM((2 * plan.m, *side), dtype),
            pltpu.VMEM((2 * plan.m, *side), dtype),
            pltpu.VMEM((blocks, *side), dtype),
            pltpu.VMEM((blocks, *side), dtype),
            pltpu.VMEM((blocks, *side), dtype),
            pltpu.VMEM((blocks + 1, *side), jnp.float32),
            pltpu.VMEM((per_dev, *side), jnp.float32),
            dma((7,)),
            dma((2 * slots,)),
            dma((2 * slots,)),
            dma((slots,)),
            dma((slots,)),
            dma((slots,)),
            dma((slots,)),
            dma((pieces,)),
            dma((pieces,)),
            dma((pieces,)),
            dma((pieces,)),
            dma,
        ],
        compiler_params=pltpu.CompilerParams(
            collective_id=0, has_side_effects=True, vmem_limit_bytes=VMEM_LIMIT
        ),
        name="gradient",
    )(*tables, scene, observed, weights, bank, psf)


def on_device(
    scene,
    observed,
    inverse_variance,
    intersection,
    resample_index,
    psf_index,
    resample_bank,
    psf_bank,
):
    owner = lax.axis_index("scene")
    strips = lax.axis_size("expo")
    strip = lax.axis_index("expo")
    per_dev = scene.shape[0]
    width = intersection.shape[1]
    kernels = resample_bank.shape[0]
    plan = Plan(lax.axis_size("scene"), intersection.shape[0])
    match = intersection // (strips * per_dev) == owner
    live = jnp.any(match, axis=1)
    place = (intersection // per_dev % strips - strip + 1) * per_dev + intersection % per_dev
    place = jnp.clip(place, 0, 3 * per_dev - 1)
    position = jnp.where(live, jnp.sum(jnp.where(match, place, 0), axis=1), per_dev)
    row = jnp.sum(jnp.where(match, resample_index[:, :width], 0), axis=1)
    row = jnp.where(live, row, kernels)
    col = jnp.sum(jnp.where(match, resample_index[:, width:], 0), axis=1)
    own = jnp.clip(position - per_dev, 0, per_dev - 1)
    low = jnp.where(position < per_dev, position, 0)
    high = jnp.maximum(position - 2 * per_dev, 0)
    give = jnp.concatenate([passed_along(low, "expo", -1), passed_along(high, "expo", 1)])
    slot = jnp.where(live, position, -1)
    turn = plan.turns(owner, slot.shape[0])
    before = (slot[:, None] == slot[None, :]) & (turn[None, :] < turn[:, None])
    prev = jnp.max(jnp.where(before, turn[None, :] + 1, 0), axis=1)
    slots = jnp.arange(3 * per_dev, dtype=jnp.int32)
    last = jnp.max(jnp.where(slots[:, None] == slot[None, :], turn[None, :] + 1, 0), axis=1)
    middle, above, below = gradient_parts(
        plan, (position, own, give, row, col, psf_index, prev, last), scene, observed, inverse_variance,
        resample_bank, psf_bank,
    )
    above = jnp.where(strip < strips - 1, above.astype(jnp.float32), 0.0)
    below = jnp.where(strip > 0, below.astype(jnp.float32), 0.0)
    return middle + above + below


def solution(mesh):
    return jax.shard_map(
        on_device,
        mesh=mesh,
        in_specs=(
            P(("scene", "expo"), None, None),
            P("expo", None, None),
            P("expo", None, None),
            P("expo", None),
            P("expo", None),
            P("expo"),
            P(),
            P(),
        ),
        out_specs=P(("scene", "expo"), None, None),
        check_vma=False,
    )
```

```python
import functools

import jax
import jax.numpy as jnp
from jax import lax
from jax.experimental import pallas as pl
from jax.experimental.pallas import tpu as pltpu
from jax.sharding import PartitionSpec as P

MESH = pl.DeviceIdType.MESH
UNROLL = 4
PIECES = 4
VMEM_LIMIT = 60 * 1024 * 1024


def dot(a, b, dims):
    return lax.dot_general(a, b, (dims, ((), ())), preferred_element_type=jnp.float32)


NN = ((1,), (0,))
NT = ((1,), (1,))
TN = ((0,), (0,))


def passed_along(value, axis, steps):
    count = lax.axis_size(axis)
    initial, last = (max(0, -steps), min(count, count - steps))
    return lax.ppermute(value, axis, [(source, source + steps) for source in range(initial, last)])


class Plan:
    def __init__(self, owners, exposures):
        self.n = owners
        self.bits = owners.bit_length() - 1
        assert 1 << self.bits == owners
        self.half = exposures // 2
        self.m = self.half // owners
        self.c = min(8, self.m)
        self.chunks = self.m // self.c

    def bit(self, h, p):
        return p if h == 0 else self.bits - 1 - p

    def value(self, owner, h, p):
        return (owner // (1 << self.bit(h, p))) % 2

    def partner(self, owner, h, p):
        step = 1 << self.bit(h, p)
        return owner + step - 2 * step * self.value(owner, h, p)

    def unit(self, owner, h, t):
        u = 0
        for p in range(self.bits):
            weight = self.n >> (p + 1)
            v = self.value(owner, h, p)
            u = u + weight * (v if t & weight else 1 - v)
        return h * self.half + u * self.m

    def base(self, h, t):
        return h * self.half + t * self.m

    def turn(self, h, t, k):
        return (((self.n - 1 - t) * self.chunks + k) * 2 + h) * self.c

    def turns(self, owner, exposures):
        j = jnp.arange(exposures, dtype=jnp.int32)
        h, u, i = j // self.half, j % self.half // self.m, j % self.m
        me = [self.unit(owner, h, self.n - 1) - h * self.half for h in range(2)]
        apart = jnp.bitwise_xor(u, jnp.where(h == 0, me[0], me[1]) // self.m)
        return ((apart * self.chunks + i // self.c) * 2 + h) * self.c + i % self.c

    def phase(self, t):
        p = 0
        while t >= self.n - (self.n >> (p + 1)):
            p += 1
        return p


def forward_kernel(
    plan, per_dev, pos_s, own_s, give_s, row_s, col_s, psf_s, prev_s, last_s, scene, observed, weights, bank_h,
    psf_h, middle_h, above_h, below_h,
    held, stage, came, bank, psf, obs, ivar, terms, got, adj, run, middle, load_sem, z_send, z_recv,
    rs_send, rs_recv, ag_send, ag_recv, lower_send, lower_recv, upper_send, upper_recv, store_sem,
):
    n, m, c = plan.n, plan.m, plan.c
    kernels = bank_h.shape[0]
    owner = lax.axis_index("scene")
    strip = lax.axis_index("expo")
    strips = lax.axis_size("expo")

    barrier = pltpu.get_barrier_semaphore()
    for p in range(plan.bits):
        pl.semaphore_signal(
            barrier, inc=1, device_id={"scene": plan.partner(owner, 0, p)}, device_id_type=MESH
        )

    @pl.when(strip > 0)
    def _():
        pl.semaphore_signal(barrier, inc=1, device_id={"expo": strip - 1}, device_id_type=MESH)

    @pl.when(strip < strips - 1)
    def _():
        pl.semaphore_signal(barrier, inc=1, device_id={"expo": strip + 1}, device_id_type=MESH)

    loads = [
        pltpu.make_async_copy(scene, held, load_sem.at[0]),
        pltpu.make_async_copy(bank_h, bank.at[pl.ds(0, kernels)], load_sem.at[1]),
        pltpu.make_async_copy(psf_h, psf, load_sem.at[2]),
    ]
    for h in range(2):
        home = plan.unit(owner, h, n - 1)
        loads.append(
            pltpu.make_async_copy(
                observed.at[pl.ds(home, m)], obs.at[pl.ds(h * m, m)], load_sem.at[3 + 2 * h]
            )
        )
        loads.append(
            pltpu.make_async_copy(
                weights.at[pl.ds(home, m)], ivar.at[pl.ds(h * m, m)], load_sem.at[4 + 2 * h]
            )
        )
    for load in loads:
        load.start()
    bank[kernels] = jnp.zeros(bank.shape[1:], bank.dtype)
    run[0] = jnp.zeros(run.shape[1:], run.dtype)

    below = jnp.where(strip > 0, 1, 0)
    above = jnp.where(strip < strips - 1, 1, 0)
    pl.semaphore_wait(barrier, plan.bits + below + above)

    blocks = terms.shape[0]

    def z_copy(up, h, t, k):
        where = (0 if up else blocks) + plan.base(h, t) + k * c
        return pltpu.make_async_remote_copy(
            src_ref=stage.at[pl.ds(where, c)],
            dst_ref=came.at[pl.ds(where, c)],
            send_sem=z_send.at[where // c],
            recv_sem=z_recv.at[where // c],
            device_id={"expo": strip + (1 if up else -1)},
            device_id_type=MESH,
        )

    loads[0].wait()
    for t in range(n):
        for k in range(plan.chunks):
            for h in range(2):
                for up in (1, 0):
                    first = (0 if up else blocks) + plan.unit(owner, h, t) + k * c
                    where = (0 if up else blocks) + plan.base(h, t) + k * c

                    def fill(i, carry, first=first, where=where):
                        stage[where + i] = held[give_s[first + i]]
                        return carry

                    lax.fori_loop(0, c, fill, 0, unroll=2)

                    @pl.when(strip < strips - 1 if up else strip > 0)
                    def _(up=up, h=h, t=t, k=k):
                        z_copy(up, h, t, k).start()

    @pl.when(strip == 0)
    def _():
        def wipe(i, carry):
            came[i] = jnp.zeros(came.shape[1:], came.dtype)
            return carry

        lax.fori_loop(0, blocks, wipe, 0)

    @pl.when(strip == strips - 1)
    def _():
        def wipe(i, carry):
            came[blocks + i] = jnp.zeros(came.shape[1:], came.dtype)
            return carry

        lax.fori_loop(0, blocks, wipe, 0)

    for load in loads[1:]:
        load.wait()

    def scatter_copy(h, t, k):
        where = plan.base(h, t) + k * c
        slot = where // c
        return pltpu.make_async_remote_copy(
            src_ref=terms.at[pl.ds(where, c)],
            dst_ref=got.at[pl.ds(where, c)],
            send_sem=rs_send.at[slot],
            recv_sem=rs_recv.at[slot],
            device_id={"scene": plan.partner(owner, h, plan.phase(t))},
            device_id_type=MESH,
        )

    def gather_copy(h, t, p, k):
        source = plan.base(h, t) + k * c
        target = plan.base(h, t - (n >> (p + 1))) + k * c
        slot = target // c
        return pltpu.make_async_remote_copy(
            src_ref=adj.at[pl.ds(source, c)],
            dst_ref=adj.at[pl.ds(target, c)],
            send_sem=ag_send.at[slot],
            recv_sem=ag_recv.at[slot],
            device_id={"scene": plan.partner(owner, h, p)},
            device_id_type=MESH,
        )

    def make_terms(h, t, k):
        where = plan.base(h, t) + k * c
        first = plan.unit(owner, h, t) + k * c

        def body(i, carry):
            for e in range(UNROLL):
                j = first + i * UNROLL + e
                position = pos_s[j]
                here = where + i * UNROLL + e
                block = lax.select(position < per_dev, came[here], held[own_s[j]])
                block = lax.select(position >= 2 * per_dev, came[blocks + here], block)
                inner = dot(block, bank[col_s[j]], NT).astype(jnp.bfloat16)
                term = dot(bank[row_s[j]], inner, NN).astype(jnp.bfloat16)
                terms[where + i * UNROLL + e] = term
            return carry

        lax.fori_loop(0, c // UNROLL, body, 0)

    def arrived(t):
        return [t - (n >> (q + 1)) for q in range(plan.bits) if t >= n - (n >> (q + 1))]

    def summed(h, t, k, i):
        total = terms[plan.base(h, t) + k * c + i].astype(jnp.float32)
        for source in arrived(t):
            total = total + got[plan.base(h, source) + k * c + i].astype(jnp.float32)
        return total.astype(jnp.bfloat16)

    def pass_on(h, t, k):
        where = plan.base(h, t) + k * c

        def body(i, carry):
            terms[where + i] = summed(h, t, k, i)
            return carry

        lax.fori_loop(0, c, body, 0)

    def psf_pass(h, k):
        where = plan.base(h, n - 1) + k * c
        first = plan.unit(owner, h, n - 1) + k * c
        here = h * m + k * c

        def body(i, carry):
            for e in range(UNROLL):
                a = i * UNROLL + e
                q = psf[psf_s[first + a]]
                half = dot(summed(h, n - 1, k, a), q, NT).astype(jnp.bfloat16)
                model = dot(q, half, NN)
                weighted = (
                    ivar[here + a].astype(jnp.float32) * (model - obs[here + a].astype(jnp.float32))
                ).astype(jnp.bfloat16)
                back = dot(weighted, q, NN).astype(jnp.bfloat16)
                adj[where + a] = dot(q, back, TN).astype(jnp.bfloat16)
            return carry

        lax.fori_loop(0, c // UNROLL, body, 0)

    for t in range(n):
        for k in range(plan.chunks):
            for h in range(2):

                @pl.when(strip > 0)
                def _(h=h, t=t, k=k):
                    z_copy(1, h, t, k).wait_recv()

                @pl.when(strip < strips - 1)
                def _(h=h, t=t, k=k):
                    z_copy(0, h, t, k).wait_recv()

                make_terms(h, t, k)
                for source in arrived(t):
                    scatter_copy(h, source, k).wait_recv()
                if t < n // 2:
                    scatter_copy(h, t, k).start()
                elif t < n - 1:
                    pass_on(h, t, k)
                    scatter_copy(h, t, k).start()
                else:
                    psf_pass(h, k)
                    for p in reversed(range(plan.bits)):
                        gather_copy(h, n - 1, p, k).start()

    for t in range(n):
        for k in range(plan.chunks):
            for h in range(2):

                @pl.when(strip < strips - 1)
                def _(h=h, t=t, k=k):
                    z_copy(1, h, t, k).wait_send()

                @pl.when(strip > 0)
                def _(h=h, t=t, k=k):
                    z_copy(0, h, t, k).wait_send()

    def pull(h, t, k):
        where = plan.base(h, t) + k * c
        first = plan.unit(owner, h, t) + k * c
        place = 1 + plan.turn(h, t, k)

        def body(i, carry):
            pulled = []
            for e in range(UNROLL):
                j = first + i * UNROLL + e
                spread = dot(adj[where + i * UNROLL + e], bank[col_s[j]], NN).astype(jnp.bfloat16)
                pulled.append(dot(bank[row_s[j]], spread, TN))
            for e in range(UNROLL):
                j = first + i * UNROLL + e
                run[place + i * UNROLL + e] = pulled[e] + run[prev_s[j]]
            return carry

        lax.fori_loop(0, c // UNROLL, body, 0)

    for k in range(plan.chunks):
        for h in range(2):
            pull(h, n - 1, k)
    for last in reversed(range(plan.bits)):
        for t in reversed(range(n - (n >> last), n - (n >> (last + 1)))):
            for k in range(plan.chunks):
                for h in range(2):
                    gather_copy(h, t + (n >> (last + 1)), last, k).wait_recv()
                    for p in reversed(range(last)):
                        gather_copy(h, t, p, k).start()
                    pull(h, t, k)

    def edge_copy(up, piece):
        out, send, recv = (
            (below_h, upper_send, upper_recv) if up else (above_h, lower_send, lower_recv)
        )
        return pltpu.make_async_remote_copy(
            src_ref=stage.at[pl.ds(up * per_dev + piece * size, size)],
            dst_ref=out.at[pl.ds(piece * size, size)],
            send_sem=send.at[piece],
            recv_sem=recv.at[piece],
            device_id={"expo": strip + (1 if up else -1)},
            device_id_type=MESH,
        )

    pieces = lower_send.shape[0]
    size = per_dev // pieces
    for piece in range(pieces):
        for up in range(2):

            def put(i, carry, up=up, piece=piece):
                a = piece * size + i
                stage[up * per_dev + a] = run[last_s[2 * up * per_dev + a]].astype(stage.dtype)
                return carry

            lax.fori_loop(0, size, put, 0, unroll=2)

            @pl.when(strip < strips - 1 if up else strip > 0)
            def _(up=up, piece=piece):
                edge_copy(up, piece).start()

    def own(i, carry):
        middle[i] = run[last_s[per_dev + i]]
        return carry

    lax.fori_loop(0, per_dev, own, 0, unroll=2)
    store = pltpu.make_async_copy(middle, middle_h, store_sem)
    store.start()

    for t in range(n - 1):
        for k in range(plan.chunks):
            for h in range(2):
                scatter_copy(h, t, k).wait_send()
                p = plan.phase(t)
                gather_copy(h, t + (n >> (p + 1)), p, k).wait_send()

    @pl.when(strip < strips - 1)
    def _():
        for piece in range(pieces):
            edge_copy(1, piece).wait_send()
            edge_copy(0, piece).wait_recv()

    @pl.when(strip > 0)
    def _():
        for piece in range(pieces):
            edge_copy(0, piece).wait_send()
            edge_copy(1, piece).wait_recv()

    store.wait()


def gradient_parts(plan, tables, scene, observed, weights, bank, psf):
    per_dev = scene.shape[0]
    blocks, side = tables[0].shape[0], scene.shape[1:]
    slots = blocks // plan.c
    pieces = PIECES
    dtype = scene.dtype
    smem = pl.BlockSpec(memory_space=pltpu.SMEM)
    hbm = pl.BlockSpec(memory_space=pl.ANY)
    dma = pltpu.SemaphoreType.DMA
    return pl.pallas_call(
        functools.partial(forward_kernel, plan, per_dev),
        out_shape=[
            jax.ShapeDtypeStruct((per_dev, *side), jnp.float32),
            jax.ShapeDtypeStruct((per_dev, *side), jnp.bfloat16),
            jax.ShapeDtypeStruct((per_dev, *side), jnp.bfloat16),
        ],
        in_specs=[smem] * len(tables) + [hbm] * 5,
        out_specs=[hbm] * 3,
        scratch_shapes=[
            pltpu.VMEM((per_dev, *side), dtype),
            pltpu.VMEM((2 * blocks, *side), dtype),
            pltpu.VMEM((2 * blocks, *side), dtype),
            pltpu.VMEM((bank.shape[0] + 1, *side), dtype),
            pltpu.VMEM(psf.shape, dtype),
            pltpu.VMEM((2 * plan.m, *side), dtype),
            pltpu.VMEM((2 * plan.m, *side), dtype),
            pltpu.VMEM((blocks, *side), dtype),
            pltpu.VMEM((blocks, *side), dtype),
            pltpu.VMEM((blocks, *side), dtype),
            pltpu.VMEM((blocks + 1, *side), jnp.float32),
            pltpu.VMEM((per_dev, *side), jnp.float32),
            dma((7,)),
            dma((2 * slots,)),
            dma((2 * slots,)),
            dma((slots,)),
            dma((slots,)),
            dma((slots,)),
            dma((slots,)),
            dma((pieces,)),
            dma((pieces,)),
            dma((pieces,)),
            dma((pieces,)),
            dma,
        ],
        compiler_params=pltpu.CompilerParams(
            collective_id=0, has_side_effects=True, vmem_limit_bytes=VMEM_LIMIT
        ),
        name="gradient",
    )(*tables, scene, observed, weights, bank, psf)


def on_device(
    scene,
    observed,
    inverse_variance,
    intersection,
    resample_index,
    psf_index,
    resample_bank,
    psf_bank,
):
    owner = lax.axis_index("scene")
    strips = lax.axis_size("expo")
    strip = lax.axis_index("expo")
    per_dev = scene.shape[0]
    width = intersection.shape[1]
    kernels = resample_bank.shape[0]
    plan = Plan(lax.axis_size("scene"), intersection.shape[0])
    match = intersection // (strips * per_dev) == owner
    live = jnp.any(match, axis=1)
    place = (intersection // per_dev % strips - strip + 1) * per_dev + intersection % per_dev
    place = jnp.clip(place, 0, 3 * per_dev - 1)
    position = jnp.where(live, jnp.sum(jnp.where(match, place, 0), axis=1), per_dev)
    row = jnp.sum(jnp.where(match, resample_index[:, :width], 0), axis=1)
    row = jnp.where(live, row, kernels)
    col = jnp.sum(jnp.where(match, resample_index[:, width:], 0), axis=1)
    own = jnp.clip(position - per_dev, 0, per_dev - 1)
    low = jnp.where(position < per_dev, position, 0)
    high = jnp.maximum(position - 2 * per_dev, 0)
    give = jnp.concatenate([passed_along(low, "expo", -1), passed_along(high, "expo", 1)])
    slot = jnp.where(live, position, -1)
    turn = plan.turns(owner, slot.shape[0])
    before = (slot[:, None] == slot[None, :]) & (turn[None, :] < turn[:, None])
    prev = jnp.max(jnp.where(before, turn[None, :] + 1, 0), axis=1)
    slots = jnp.arange(3 * per_dev, dtype=jnp.int32)
    last = jnp.max(jnp.where(slots[:, None] == slot[None, :], turn[None, :] + 1, 0), axis=1)
    middle, above, below = gradient_parts(
        plan, (position, own, give, row, col, psf_index, prev, last), scene, observed, inverse_variance,
        resample_bank, psf_bank,
    )
    above = jnp.where(strip < strips - 1, above.astype(jnp.float32), 0.0)
    below = jnp.where(strip > 0, below.astype(jnp.float32), 0.0)
    return middle + above + below


def solution(mesh):
    return jax.shard_map(
        on_device,
        mesh=mesh,
        in_specs=(
            P(("scene", "expo"), None, None),
            P("expo", None, None),
            P("expo", None, None),
            P("expo", None),
            P("expo", None),
            P("expo"),
            P(),
            P(),
        ),
        out_specs=P(("scene", "expo"), None, None),
        check_vma=False,
    )
```
